512 devices in a mesh: seq: 128 (over z, x_hi, y), head: 4 (over x_lo, core).
Axes of the slice: x: 4 (x_hi: 2, x_lo: 2; x = x_hi * 2 + x_lo), y: 8, z: 8, core: 2. Of those that a mesh axis runs over, the one named last changes fastest.
Arguments:
- qkv: bfloat16 [2, 3, 16384, 8, 128], P(None, None, 'seq', 'head'), may hold values from -48 to 48
- out_weight: bfloat16 [2, 8, 128, 2048], P(None, 'head'), may hold values from -0.59765625 to 0.59765625
- out_grad: bfloat16 [16384, 2048], P('seq', 'head'), may hold values from -6 to 6
Outputs:
- mixed: bfloat16 [16384, 2048], P('seq', 'head')
- grads: bfloat16 [2, 3, 16384, 8, 128], P(None, None, 'seq', 'head')
The draws below stay inside these ranges and needn't reach their ends.
All inputs are finite; a program needn't handle non-finite values.
Results may differ from the reference program's by a relative error of at most 0.039.
Values may be sent and summed in bfloat16 or wider, within the bound.
No kernel may reach another device: no remote copies, remote signals or barrier semaphores. Data moves between devices by JAX's collectives and lax.ppermute only.
A program may use at most 64 MiB of HBM per device.

```python
import math
import jax
import jax.numpy as jnp
from jax import lax

HD = 128
HK = 8
D = 2048
ROW = 512
TOKENS = 16384


def draw_qkv(key, part):
    streams = jax.random.split(key, 1)
    shape = (2, 3, TOKENS, HK, HD)
    base = jnp.clip(jax.random.normal(streams[0], shape, jnp.float32), -4.0, 4.0)
    return base.astype(jnp.bfloat16)


def level_of(own_key, dims, shards, low, high):
    factor_of = 1.0
    for axis_at, parts in shards:
        draws = jax.random.uniform(jax.random.fold_in(jax.random.fold_in(own_key, 6), axis_at), (parts,), jnp.float32, low / len(shards), high / len(shards))
        factor_of = factor_of * jnp.repeat(jnp.exp(draws), dims[axis_at] // parts).reshape((-1,) + (1,) * (len(dims) - 1 - axis_at))
    return factor_of


def scatter_about(stream_key, extent, deviation, bound, shards=(), kind=jnp.bfloat16):
    gain = level_of(stream_key, extent, shards, -0.22, 0.18) if shards else 1.0
    drawn = jax.random.normal(stream_key, extent, jnp.float32) * deviation * gain
    return jnp.minimum(jnp.maximum(drawn, -bound), bound).astype(kind)


def setup_inputs(seed: int = 0) -> dict:
    key_list = jax.random.split(jax.random.key(seed), 4)
    return {
        "qkv": draw_qkv(jax.random.fold_in(key_list[3], 71), 0),
        "out_weight": scatter_about(key_list[1], (2, HK, HD, D), 0.1, 0.59765625, ((1, 4),)),
        "out_grad": scatter_about(key_list[2], (TOKENS, D), 1.0, 6.0, ((0, 128), (1, 4))),
    }


def rounded(values):
    return lax.optimization_barrier(values.astype(jnp.bfloat16)).astype(jnp.float32)

def masked_softmax(scores, allowed):
    largest = lax.optimization_barrier(jnp.max(jnp.where(allowed, scores, -jnp.inf), axis=-1, keepdims=True))
    raised = jnp.exp(jnp.where(allowed, scores - largest, -jnp.inf))
    totals = lax.optimization_barrier(jnp.sum(raised, axis=-1, keepdims=True))
    return (raised / totals, largest + jnp.log(totals))

def band_mask(query_pos, key_pos):
    apart = query_pos[:, None] - key_pos[None, :]
    return (apart >= 0) & (apart < ROW) & (key_pos[None, :] >= 0)

def reference(qkv, out_weight, out_grad):
    score_scale = 1.0 / math.sqrt(HD)
    line_count = TOKENS // ROW
    local_part = qkv[0].astype(jnp.float32)
    padded = jnp.pad(local_part[1:3], ((0, 0), (ROW, 0), (0, 0), (0, 0)))
    weight_full = out_weight.astype(jnp.float32)
    grad_heads = rounded(jnp.einsum('to,khdo->kthd', out_grad.astype(jnp.float32), weight_full))
    grad_local = grad_heads[0]

    def band_inputs(index):
        first = index * ROW
        query = lax.dynamic_slice_in_dim(local_part[0], first, ROW, 0)
        pairs = lax.dynamic_slice_in_dim(padded, first, 2 * ROW, 1)
        query_pos = first + jnp.arange(ROW, dtype=jnp.int32)
        key_pos = first - ROW + jnp.arange(2 * ROW, dtype=jnp.int32)
        scores = jnp.einsum('thd,shd->hts', query, pairs[0]) * score_scale
        return (query, pairs, scores, band_mask(query_pos, key_pos)[None])

    def band_forward(index):
        query, pairs, scores, allowed = band_inputs(index)
        weights, lse = masked_softmax(scores, allowed)
        attended = rounded(jnp.einsum('hts,shd->thd', rounded(weights), pairs[1]))
        return (attended, lse)
    indices = jnp.arange(line_count, dtype=jnp.int32)
    band_out, band_lse = lax.map(band_forward, indices)
    strided_part = qkv[1].astype(jnp.float32).reshape(3, line_count, ROW, HK, HD)
    line_idx = jnp.arange(line_count, dtype=jnp.int32)
    causal = line_idx[:, None] >= line_idx[None, :]
    col_scores = jnp.einsum('rchd,uchd->chru', strided_part[0], strided_part[1]) * score_scale
    col_weights, col_lse = masked_softmax(col_scores, causal)
    col_out = rounded(jnp.einsum('chru,uchd->rchd', rounded(col_weights), strided_part[2]))
    local_out = band_out.reshape(TOKENS, HK, HD)
    strided_out = col_out.reshape(TOKENS, HK, HD)
    mixed = (jnp.einsum('thd,hdo->to', local_out, weight_full[0]) + jnp.einsum('thd,hdo->to', strided_out, weight_full[1])).astype(jnp.bfloat16)

    def band_backward(index):
        query, pairs, scores, allowed = band_inputs(index)
        grad_o = lax.dynamic_slice_in_dim(grad_local, index * ROW, ROW, 0)
        attended = band_out[index]
        delta = jnp.einsum('thd,thd->ht', grad_o, attended)
        probs = jnp.exp(jnp.where(allowed, scores - band_lse[index], -jnp.inf))
        grad_p = jnp.einsum('thd,shd->hts', grad_o, pairs[1])
        grad_s = rounded(probs * (grad_p - delta[..., None]))
        grad_query = rounded(jnp.einsum('hts,shd->thd', grad_s, pairs[0]) * score_scale)
        grad_key = jnp.einsum('hts,thd->shd', grad_s, query) * score_scale
        grad_value = jnp.einsum('hts,thd->shd', rounded(probs), grad_o)
        return (grad_query, grad_key, grad_value)
    grad_query, grad_key, grad_value = lax.map(band_backward, indices)

    def combine(pieces):
        follow = jnp.concatenate([pieces[1:, :ROW], jnp.zeros_like(pieces[:1, :ROW])], axis=0)
        return (pieces[:, ROW:] + follow).reshape(TOKENS, HK, HD)
    local_grads = jnp.stack([grad_query.reshape(TOKENS, HK, HD), combine(grad_key), combine(grad_value)])
    grad_col = grad_heads[1].reshape(line_count, ROW, HK, HD)
    col_delta = jnp.einsum('rchd,rchd->chr', grad_col, col_out)
    col_probs = jnp.exp(jnp.where(causal, col_scores - col_lse, -jnp.inf))
    col_gp = jnp.einsum('rchd,uchd->chru', grad_col, strided_part[2])
    col_gs = rounded(col_probs * (col_gp - col_delta[..., None]))
    strided_dq = rounded(jnp.einsum('chru,uchd->rchd', col_gs, strided_part[1]) * score_scale)
    strided_dk = rounded(jnp.einsum('chru,rchd->uchd', col_gs, strided_part[0]) * score_scale)
    strided_dv = rounded(jnp.einsum('chru,rchd->uchd', rounded(col_probs), grad_col))
    strided_grads = jnp.stack([strided_dq, strided_dk, strided_dv]).reshape(3, TOKENS, HK, HD)
    grads = jnp.stack([local_grads.astype(jnp.bfloat16), strided_grads.astype(jnp.bfloat16)])
    return (mixed, grads)
```

```python
import math

import jax
import jax.numpy as jnp
from jax import lax
from jax.experimental import pallas as pl
from jax.experimental.pallas import tpu as pltpu
from jax.sharding import Mesh
from jax.sharding import PartitionSpec as P

ROW = 512
F32 = jnp.float32
BF16 = jnp.bfloat16


def dot(a, b, dims):
    return lax.dot_general(a, b, (dims, ((), ())), preferred_element_type=F32)


def mm(a, b):
    return dot(a, b, ((1,), (0,)))


def mm_nt(a, b):
    return dot(a, b, ((1,), (1,)))


def mm_tn(a, b):
    return dot(a, b, ((0,), (0,)))


def iota(shape, axis):
    return lax.broadcasted_iota(jnp.int32, shape, axis)


def attend(q, k, v, g, allowed, scale):
    scores = jnp.where(allowed, mm_nt(q, k) * scale, -jnp.inf)
    largest = jnp.max(scores, axis=1, keepdims=True)
    raised = jnp.exp(scores - largest)
    probs = raised / jnp.sum(raised, axis=1, keepdims=True)
    rounded = probs.astype(BF16)
    out = mm(rounded, v).astype(BF16)
    delta = jnp.sum(g.astype(F32) * out.astype(F32), axis=1, keepdims=True)
    gs = (probs * (mm_nt(g, v) - delta)).astype(BF16)
    return out, mm(gs, k) * scale, mm_tn(gs, q) * scale, mm_tn(rounded, g)


def grad_heads_kernel(og_ref, w_ref, qkv_ref, send_ref, local_ref):
    parts, _, width = og_ref.shape
    g = sum(
        mm_nt(og_ref[p], w_ref[:, p * width : (p + 1) * width]) for p in range(parts)
    ).astype(BF16)
    rows, hd = local_ref.shape
    tokens = g.shape[0]
    heads = rows // tokens
    lines, _, span, _ = send_ref.shape

    def interleave(first):
        total = 0
        for h in range(heads):
            pick = iota((rows, tokens), 0) == heads * iota((rows, tokens), 1) + h
            at = (first + h) * hd
            total = total + mm(pick.astype(BF16), g[:, at : at + hd])
        return total

    local_ref[...] = interleave(0).astype(BF16)
    send_ref[:, 3] = interleave(heads).reshape(lines, span, hd).astype(BF16)
    for kind in range(3):
        send_ref[:, kind] = qkv_ref[0, kind].astype(F32).reshape(lines, span, hd).astype(BF16)


def strided_kernel(heads, scale, in_ref, out_ref):
    lines, _, span, hd = in_ref.shape
    rows = lines * span

    def part(kind):
        return in_ref[:, kind].astype(F32).reshape(rows, hd).astype(BF16)

    at, to = iota((rows, rows), 0), iota((rows, rows), 1)
    allowed = (at >= to) & (at % span == to % span)
    results = attend(part(0), part(1), part(2), part(3), allowed, scale)
    for kind, value in enumerate(results):
        out_ref[:, kind] = value.astype(F32).reshape(lines, span, hd).astype(BF16)


def local_kernel(back, heads, scale, rank_ref, qkv_ref, g_ref, *refs):
    far = refs[:back]
    out_ref, dq_ref, own_ref = refs[back : back + 3]
    far_out = refs[back + 3 :]
    rows = g_ref.shape[0]
    tokens = rows // heads
    keys = jnp.concatenate([r[0] for r in far] + [qkv_ref[0, 1]], axis=0)
    values = jnp.concatenate([r[1] for r in far] + [qkv_ref[0, 2]], axis=0)
    shape = (rows, (back + 1) * rows)
    at, to = iota(shape, 0), iota(shape, 1)
    apart = at // heads + back * tokens - to // heads
    first = (back - rank_ref[0]) * rows
    allowed = (apart >= 0) & (apart < ROW) & (at % heads == to % heads) & (to >= first)
    out, dq, dk, dv = attend(qkv_ref[0, 0], keys, values, g_ref[...], allowed, scale)
    out_ref[...] = out
    dq_ref[...] = dq.astype(BF16)
    own_ref[0] = dk[back * rows :]
    own_ref[1] = dv[back * rows :]
    for j, ref in enumerate(far_out):
        ref[0] = dk[j * rows : (j + 1) * rows].astype(BF16)
        ref[1] = dv[j * rows : (j + 1) * rows].astype(BF16)


def project_kernel(heads, local_ref, back_ref, w_ref, out_ref):
    rows, hd = local_ref.shape
    tokens = rows // heads
    parts, _, width = out_ref.shape
    strided = back_ref[:, 0].astype(F32).reshape(rows, hd).astype(BF16)
    pieces = []
    for value in (local_ref[...], strided):
        for h in range(heads):
            pick = iota((tokens, rows), 1) == heads * iota((tokens, rows), 0) + h
            pieces.append(mm(pick.astype(BF16), value).astype(BF16))
    attended = jnp.concatenate(pieces, axis=1)
    for p in range(parts):
        out_ref[p] = mm(attended, w_ref[:, p * width : (p + 1) * width]).astype(BF16)


def finish_kernel(sums_ref, dq_ref, own_ref, back_ref, *refs):
    far, mixed_ref, grads_ref = refs[:-2], refs[-2], refs[-1]
    mixed_ref[...] = sum(sums_ref[p].astype(F32) for p in range(sums_ref.shape[0])).astype(BF16)
    rows, hd = dq_ref.shape
    grads_ref[0, 0] = dq_ref[...]
    for kind in range(2):
        total = own_ref[kind] + sum(r[kind].astype(F32) for r in far)
        grads_ref[0, 1 + kind] = total.astype(BF16)
    for kind in range(3):
        grads_ref[1, kind] = back_ref[:, 1 + kind].astype(F32).reshape(rows, hd).astype(BF16)


def call(kernel, outs, *args, in_specs=None, name=None):
    kw = {} if in_specs is None else {"in_specs": in_specs, "grid": (1,)}
    single = not isinstance(outs, (list, tuple))
    listed = [outs] if single else list(outs)
    if in_specs is not None:
        kw["out_specs"] = [pl.BlockSpec(o.shape, lambda i, n=len(o.shape): (0,) * n) for o in listed]
    res = pl.pallas_call(kernel, out_shape=listed, name=name, **kw)(*args)
    return res[0] if single else res


def whole(a):
    return pl.BlockSpec(a.shape, lambda i, n=len(a.shape): (0,) * n)


def shards(qkv, out_weight, out_grad):
    _, _, tokens, heads, hd = qkv.shape
    lines = lax.axis_size("line")
    quarters = lax.axis_size("quarter")
    parts = lax.axis_size("head")
    seq = ("line", "quarter")
    count = lines * quarters
    rank = (lax.axis_index("line") * quarters + lax.axis_index("quarter")).astype(jnp.int32)
    scale = 1.0 / math.sqrt(hd)
    back = (ROW - 1) // tokens + 1
    rows = tokens * heads
    span = rows // lines
    width = out_grad.shape[1]
    shape = jax.ShapeDtypeStruct

    def shifted(value, steps):
        pairs = [(i, i + steps) for i in range(count) if 0 <= i + steps < count]
        return lax.ppermute(value, seq, pairs)

    x = qkv.reshape(2, 3, rows, hd)
    w = out_weight.reshape(2 * heads * hd, parts * width)
    kind_of = lambda k: pl.BlockSpec((1, 3, rows, hd), lambda i: (k, 0, 0, 0))

    pair = x[0, 1:3]
    far = [shifted(pair, back - j) for j in range(back)]
    og = lax.all_gather(out_grad, "head", axis=0)
    send, g_local = call(
        grad_heads_kernel,
        [shape((lines, 4, span, hd), BF16), shape((rows, hd), BF16)],
        og,
        w,
        x,
        in_specs=[whole(og), whole(w), kind_of(1)],
        name="grad_heads",
    )
    got = lax.all_to_all(send, "line", 0, 0, tiled=True)

    def local(*args):
        return local_kernel(back, heads, scale, *args)

    pair_shape = (2, rows, hd)
    local_out, local_dq, own, *far_grads = call(
        local,
        [shape((rows, hd), BF16), shape((rows, hd), BF16), shape(pair_shape, F32)]
        + [shape(pair_shape, BF16)] * back,
        rank.reshape(1),
        x,
        g_local,
        *far,
        in_specs=[pl.BlockSpec(memory_space=pltpu.SMEM), kind_of(0), whole(g_local)]
        + [whole(f) for f in far],
        name="local",
    )
    near = [shifted(far_grads[j], j - back) for j in range(back)]

    def strided(*args):
        return strided_kernel(heads, scale, *args)

    results = call(strided, shape(got.shape, BF16), got, name="strided")
    returned = lax.all_to_all(results, "line", 0, 0, tiled=True)

    def project(*args):
        return project_kernel(heads, *args)

    partial = call(project, shape((parts, tokens, width), BF16), local_out, returned, w, name="project")
    sums = lax.all_to_all(partial, "head", 0, 0, tiled=True)
    mixed, grads = call(
        finish_kernel,
        [shape((tokens, width), BF16), shape((2, 3, rows, hd), BF16)],
        sums,
        local_dq,
        own,
        returned,
        *near,
        name="finish",
    )
    return mixed, grads.reshape(qkv.shape)


def solution(mesh):
    count = mesh.shape["seq"]
    split = Mesh(
        mesh.devices.reshape(count // 4, 4, mesh.shape["head"]), ("line", "quarter", "head")
    )
    seq = ("line", "quarter")
    return jax.shard_map(
        shards,
        mesh=split,
        in_specs=(
            P(None, None, seq, "head", None),
            P(None, "head", None, None),
            P(seq, "head"),
        ),
        out_specs=(P(seq, "head"), P(None, None, seq, "head", None)),
        check_vma=False,
    )
```

```python
import functools
import math

import jax
import jax.numpy as jnp
from jax import lax
from jax.experimental import pallas as pl
from jax.experimental.pallas import tpu as pltpu
from jax.sharding import Mesh
from jax.sharding import PartitionSpec as P

ROW = 512
SCRATCH = 24 * 2**20
F32 = jnp.float32
BF16 = jnp.bfloat16


def dot(a, b, dims):
    return lax.dot_general(a, b, (dims, ((), ())), preferred_element_type=F32)


def mm(a, b):
    return dot(a, b, ((1,), (0,)))


def mm_nt(a, b):
    return dot(a, b, ((1,), (1,)))


def mm_tn(a, b):
    return dot(a, b, ((0,), (0,)))


def iota(shape, axis):
    return lax.broadcasted_iota(jnp.int32, shape, axis)


def attend(q, k, v, g, allowed, scale):
    scores = jnp.where(allowed, mm_nt(q, k) * scale, -jnp.inf)
    largest = jnp.max(scores, axis=1, keepdims=True)
    raised = jnp.exp(scores - largest)
    probs = raised * (1.0 / jnp.sum(raised, axis=1, keepdims=True))
    rounded = probs.astype(BF16)
    out = mm(rounded, v).astype(BF16)
    delta = jnp.sum(g.astype(F32) * out.astype(F32), axis=1, keepdims=True)
    gs = (probs * (mm_nt(g, v) - delta)).astype(BF16)
    return out, mm(gs, k) * scale, mm_tn(gs, q) * scale, mm_tn(rounded, g)


def rows_of(g, rows, heads, hd, tokens):
    total = 0
    for h in range(heads):
        pick = iota((rows, tokens), 0) == heads * iota((rows, tokens), 1) + h
        total = total + mm_nt(pick.astype(BF16), g[h * hd : (h + 1) * hd])
    return total


def grad_heads_kernel(heads, og_ref, w_ref, x_ref, send_ref, w_mem, x_mem, sems):
    lines, _, span, hd = send_ref.shape
    parts, tokens, width = og_ref.shape
    loads = [
        pltpu.make_async_copy(
            w_ref.at[heads * hd :, p * width : (p + 1) * width], w_mem.at[p], sems.at[p]
        )
        for p in range(parts)
    ]
    loads.append(pltpu.make_async_copy(x_ref.at[1], x_mem, sems.at[parts]))
    for load in loads:
        load.start()
    g = 0
    for p in range(parts):
        loads[p].wait()
        g = g + mm_nt(w_mem[p], og_ref[p])
    g = rows_of(g.astype(BF16), lines * span, heads, hd, tokens)
    send_ref[:, 3] = g.reshape(lines, span, hd).astype(BF16)
    loads[parts].wait()
    for kind in range(3):
        send_ref[:, kind] = x_mem[kind].astype(F32).reshape(lines, span, hd).astype(BF16)


def strided_kernel(scale, in_ref, out_ref):
    lines, _, span, hd = in_ref.shape
    rows = lines * span

    def part(kind):
        return in_ref[:, kind].astype(F32).reshape(rows, hd).astype(BF16)

    at, to = iota((rows, rows), 0), iota((rows, rows), 1)
    allowed = (at >= to) & (at % span == to % span)
    results = attend(part(0), part(1), part(2), part(3), allowed, scale)
    for kind, value in enumerate(results):
        out_ref[:, kind] = value.astype(F32).reshape(lines, span, hd).astype(BF16)


def by_token(value, heads):
    rows, _ = value.shape
    shape = (rows // heads, rows)
    picks = [iota(shape, 1) == heads * iota(shape, 0) + h for h in range(heads)]
    return jnp.concatenate([mm(p.astype(BF16), value).astype(BF16) for p in picks], axis=1)


def local_kernel(
    heads, scale, rank_ref, x_ref, og_ref, w_ref, a_ref, b_ref, c_ref,
    three_ref, four_ref, attended_ref, dq_ref, mid_ref, two_ref, one_ref,
    attended_mem, dq_mem, mid_mem, two_mem, one_mem, sems,
):
    rows, hd = dq_ref.shape
    tokens = rows // heads
    parts, _, width = og_ref.shape
    g = sum(
        mm_nt(w_ref[: heads * hd, p * width : (p + 1) * width], og_ref[p]) for p in range(parts)
    ).astype(BF16)
    same = (iota((tokens, tokens), 0) == iota((tokens, tokens), 1)).astype(BF16)

    at = iota((rows, 1), 0)
    apart = (iota((rows, rows), 1) == at % tokens * heads + at // tokens).astype(BF16)

    def split(first, second):
        return mm(apart, jnp.concatenate([first, second], axis=1)).astype(BF16)

    def joined(first, second):
        both = jnp.concatenate([first.astype(BF16), second.astype(BF16)], axis=1)
        both = mm_tn(apart, both).astype(BF16)
        return both[:, :hd], both[:, hd:]

    query = mm(apart, x_ref[0, 0]).astype(BF16)
    shards = [
        split(c_ref[0], c_ref[1]),
        split(b_ref[1, 0], b_ref[1, 1]),
        split(a_ref[0], a_ref[1]),
        split(b_ref[0, 0], b_ref[0, 1]),
        split(x_ref[0, 1], x_ref[0, 2]),
    ]
    back = ROW // tokens
    shape = (tokens, (back + 1) * tokens)
    to = iota(shape, 1)
    gap = iota((tokens, 1), 0) + back * tokens - to
    first = (back - rank_ref[0]) * tokens
    allowed = (gap >= 0) & (gap < ROW) & (to >= first)
    results = []
    for h in range(heads):
        mine = slice(h * tokens, (h + 1) * tokens)
        keys = jnp.concatenate([s[mine, :hd] for s in shards], axis=0)
        values = jnp.concatenate([s[mine, hd:] for s in shards], axis=0)
        own_g = mm_nt(same, g[h * hd : (h + 1) * hd]).astype(BF16)
        results.append(attend(query[mine], keys, values, own_g, allowed, scale))
    outs, dqs, dks, dvs = zip(*results)
    attended_mem[...] = jnp.concatenate(outs, axis=1)
    dq_mem[...] = mm_tn(apart, jnp.concatenate(dqs, axis=0).astype(BF16)).astype(BF16)
    blocks = []
    for j in range(back + 1):
        mine = slice(j * tokens, (j + 1) * tokens)
        blocks.append(
            joined(*(jnp.concatenate([v[mine] for v in each], axis=0) for each in (dks, dvs)))
        )
    four, three, two, one, mid = blocks
    for kind in range(2):
        mid_mem[kind] = mid[kind]
        two_mem[kind] = two[kind]
        one_mem[kind] = one[kind]
        three_ref[kind] = three[kind]
        four_ref[kind] = four[kind]
    pairs = (
        (attended_mem, attended_ref),
        (dq_mem, dq_ref),
        (mid_mem, mid_ref),
        (two_mem, two_ref),
        (one_mem, one_ref),
    )
    stores = [pltpu.make_async_copy(m, r, sems.at[n]) for n, (m, r) in enumerate(pairs)]
    for store in stores:
        store.start()
    for store in stores:
        store.wait()


def project_kernel(heads, attended_ref, back_ref, w_ref, out_ref, attended_mem, sem):
    load = pltpu.make_async_copy(attended_ref, attended_mem, sem.at[0])
    load.start()
    lines, _, span, hd = back_ref.shape
    parts, _, width = out_ref.shape
    strided = by_token(back_ref[:, 0].astype(F32).reshape(lines * span, hd).astype(BF16), heads)
    load.wait()
    attended = jnp.concatenate([attended_mem[...], strided], axis=1)
    for p in range(parts):
        out_ref[p] = mm(attended, w_ref[:, p * width : (p + 1) * width]).astype(BF16)


def finish_kernel(sums_ref, dq_ref, mid_ref, *refs):
    *returns, back_ref, mixed_ref, grads_ref = refs
    mixed_ref[...] = sum(sums_ref[p].astype(F32) for p in range(sums_ref.shape[0])).astype(BF16)
    rows, hd = dq_ref.shape
    grads_ref[0, 0] = dq_ref[...]
    for kind in range(2):
        total = mid_ref[kind].astype(F32) + sum(r[kind].astype(F32) for r in returns)
        grads_ref[0, 1 + kind] = total.astype(BF16)
    for kind in range(3):
        grads_ref[1, kind] = back_ref[:, 1 + kind].astype(F32).reshape(rows, hd).astype(BF16)


def call(kernel, outs, *args, far=(), away=(), scratch=()):
    vmem, smem, hbm = [pl.BlockSpec(memory_space=m) for m in (pltpu.VMEM, pltpu.SMEM, pltpu.HBM)]
    ins = [smem if a.dtype == jnp.int32 else hbm if n in far else vmem for n, a in enumerate(args)]
    args = [
        pltpu.with_memory_space_constraint(a, pltpu.HBM) if n in far else a
        for n, a in enumerate(args)
    ]
    made = [(pltpu.HBM if n in away else jax.ShapeDtypeStruct)(*o) for n, o in enumerate(outs)]
    return pl.pallas_call(
        kernel,
        out_shape=made,
        in_specs=ins,
        out_specs=[hbm if n in away else vmem for n in range(len(outs))],
        scratch_shapes=[
            pltpu.VMEM(*s) if isinstance(s, tuple) else pltpu.SemaphoreType.DMA((s,)) for s in scratch
        ],
        compiler_params=pltpu.CompilerParams(vmem_limit_bytes=SCRATCH),
    )(*args)


def layer(qkv, out_weight, out_grad):
    _, _, tokens, heads, hd = qkv.shape
    lines = lax.axis_size("line")
    quarters = lax.axis_size("quarter")
    parts = lax.axis_size("head")
    seq = ("line", "quarter")
    count = lines * quarters
    rank = (lax.axis_index("line") * quarters + lax.axis_index("quarter")).astype(jnp.int32)
    scale = 1.0 / math.sqrt(hd)
    rows = tokens * heads
    span = rows // lines
    width = out_grad.shape[1]
    kernel = functools.partial

    def shifted(value, steps):
        pairs = [(i, i + steps) for i in range(count) if 0 <= i + steps < count]
        return lax.ppermute(value, seq, pairs)

    x = qkv.reshape(2, 3, rows, hd)
    w = out_weight.reshape(2 * heads * hd, parts * width)

    pair = x[0, 1:3]
    a = shifted(pair, 2)
    og = lax.all_gather(out_grad, "head", axis=0)
    both = jnp.stack([lax.optimization_barrier((x, a))[0][0, 1:3], a])
    b = shifted(both, 1)
    c = shifted(a, 2)
    (send,) = call(
        kernel(grad_heads_kernel, heads),
        [((lines, 4, span, hd), BF16)],
        og,
        w,
        x,
        far=(1, 2),
        scratch=(((parts, heads * hd, width), BF16), ((3, rows, hd), BF16), parts + 1),
    )
    got = lax.all_to_all(send, "line", 0, 0, tiled=True)
    flat, pair_of = (rows, hd), (2, rows, hd)
    flat, pair_of, wide = (rows, hd), (2, rows, hd), (tokens, heads * hd)
    away = (wide, flat, pair_of, pair_of, pair_of)
    three, four, attended, local_dq, mid, two, one = call(
        kernel(local_kernel, heads, scale),
        [(o, BF16) for o in (pair_of, pair_of, *away)],
        rank.reshape(1),
        x,
        og,
        w,
        a,
        b,
        c,
        away=(2, 3, 4, 5, 6),
        scratch=(*((o, BF16) for o in away), len(away)),
    )
    returns = [shifted(v, -n) for n, v in ((1, one), (2, two), (3, three), (4, four))]
    (results,) = call(kernel(strided_kernel, scale), [(got.shape, BF16)], got)
    returned = lax.all_to_all(results, "line", 0, 0, tiled=True)
    (partial,) = call(
        kernel(project_kernel, heads),
        [((parts, tokens, width), BF16)],
        attended,
        returned,
        w,
        far=(0,),
        scratch=((wide, BF16), 1),
    )
    sums = lax.all_to_all(partial, "head", 0, 0, tiled=True)
    mixed, grads = call(
        finish_kernel,
        [((tokens, width), BF16), ((2, 3, rows, hd), BF16)],
        sums,
        local_dq,
        mid,
        *returns,
        returned,
    )
    return mixed, grads.reshape(qkv.shape)


def solution(mesh):
    count = mesh.shape["seq"]
    split = Mesh(
        mesh.devices.reshape(count // 4, 4, mesh.shape["head"]), ("line", "quarter", "head")
    )
    seq = ("line", "quarter")
    return jax.shard_map(
        layer,
        mesh=split,
        in_specs=(
            P(None, None, seq, "head", None),
            P(None, "head", None, None),
            P(seq, "head"),
        ),
        out_specs=(P(seq, "head"), P(None, None, seq, "head", None)),
        check_vma=False,
    )
```

```python
import functools
import math

import jax
import jax.numpy as jnp
from jax import lax
from jax.experimental import pallas as pl
from jax.experimental.pallas import tpu as pltpu
from jax.sharding import Mesh
from jax.sharding import PartitionSpec as P

ROW = 512
SCRATCH = 24 * 2**20
F32 = jnp.float32
BF16 = jnp.bfloat16


def dot(a, b, dims):
    return lax.dot_general(a, b, (dims, ((), ())), preferred_element_type=F32)


def mm(a, b):
    return dot(a, b, ((1,), (0,)))


def mm_nt(a, b):
    return dot(a, b, ((1,), (1,)))


def mm_tn(a, b):
    return dot(a, b, ((0,), (0,)))


def iota(shape, axis):
    return lax.broadcasted_iota(jnp.int32, shape, axis)


def attend(q, k, v, g, allowed, scale):
    scores = jnp.where(allowed, mm_nt(q, k) * scale, -jnp.inf)
    largest = jnp.max(scores, axis=1, keepdims=True)
    raised = jnp.exp(scores - largest)
    probs = raised * (1.0 / jnp.sum(raised, axis=1, keepdims=True))
    rounded = probs.astype(BF16)
    out = mm(rounded, v).astype(BF16)
    delta = jnp.sum(g.astype(F32) * out.astype(F32), axis=1, keepdims=True)
    gs = (probs * (mm_nt(g, v) - delta)).astype(BF16)
    return out, mm(gs, k) * scale, mm_tn(gs, q) * scale, mm_tn(rounded, g)


def rows_of(g, rows, heads, hd, tokens):
    total = 0
    for h in range(heads):
        pick = iota((rows, tokens), 0) == heads * iota((rows, tokens), 1) + h
        total = total + mm_nt(pick.astype(BF16), g[h * hd : (h + 1) * hd])
    return total


def grad_heads_kernel(heads, og_ref, w_ref, x_ref, send_ref, w_mem, x_mem, sems):
    lines, _, span, hd = send_ref.shape
    parts, tokens, width = og_ref.shape
    loads = [
        pltpu.make_async_copy(
            w_ref.at[heads * hd :, p * width : (p + 1) * width], w_mem.at[p], sems.at[p]
        )
        for p in range(parts)
    ]
    loads.append(pltpu.make_async_copy(x_ref.at[1], x_mem, sems.at[parts]))
    for load in loads:
        load.start()
    loads[parts].wait()
    for kind in range(3):
        send_ref[:, kind] = x_mem[kind].astype(F32).reshape(lines, span, hd).astype(BF16)
    g = 0
    for p in range(parts):
        loads[p].wait()
        g = g + mm_nt(w_mem[p], og_ref[p])
    g = rows_of(g.astype(BF16), lines * span, heads, hd, tokens)
    send_ref[:, 3] = g.reshape(lines, span, hd).astype(BF16)


def strided_kernel(scale, in_ref, out_ref):
    lines, _, span, hd = in_ref.shape
    rows = lines * span

    def part(kind):
        return in_ref[:, kind].astype(F32).reshape(rows, hd).astype(BF16)

    at, to = iota((rows, rows), 0), iota((rows, rows), 1)
    allowed = (at >= to) & (at % span == to % span)
    results = attend(part(0), part(1), part(2), part(3), allowed, scale)
    for kind, value in enumerate(results):
        out_ref[:, kind] = value.astype(F32).reshape(lines, span, hd).astype(BF16)


def by_token(value, heads):
    rows, _ = value.shape
    shape = (rows // heads, rows)
    picks = [iota(shape, 1) == heads * iota(shape, 0) + h for h in range(heads)]
    return jnp.concatenate([mm(p.astype(BF16), value).astype(BF16) for p in picks], axis=1)


def places(rows, heads):
    tokens = rows // heads
    at = iota((rows, 1), 0)
    return (iota((rows, rows), 1) == at % tokens * heads + at // tokens).astype(BF16)


def split_kernel(heads, x_ref, pair_ref, query_ref, x_mem, sem):
    load = pltpu.make_async_copy(x_ref.at[0], x_mem, sem.at[0])
    load.start()
    rows, hd = query_ref.shape
    apart = places(rows, heads)
    load.wait()
    whole = mm(apart, jnp.concatenate([x_mem[k] for k in range(3)], axis=1)).astype(BF16)
    query_ref[...] = whole[:, :hd]
    pair_ref[0] = whole[:, hd : 2 * hd]
    pair_ref[1] = whole[:, 2 * hd :]


def local_grad_kernel(heads, og_ref, w_ref, g_ref):
    parts, tokens, width = og_ref.shape
    hd = g_ref.shape[1]
    g = sum(
        mm_nt(w_ref[: heads * hd, p * width : (p + 1) * width], og_ref[p]) for p in range(parts)
    ).astype(BF16)
    same = (iota((tokens, tokens), 0) == iota((tokens, tokens), 1)).astype(BF16)
    for h in range(heads):
        own = mm_nt(same, g[h * hd : (h + 1) * hd])
        g_ref[h * tokens : (h + 1) * tokens] = own.astype(BF16)


def local_kernel(
    heads, scale, rank_ref, query_ref, pair_ref, g_ref, a_ref, b_ref, c_ref,
    one_three_ref, four_ref, attended_ref, dq_ref, mid_ref, two_ref,
    attended_mem, dq_mem, mid_mem, two_mem, sems,
):
    rows, _ = dq_ref.shape
    tokens = rows // heads
    back = ROW // tokens
    shape = (tokens, (back + 1) * tokens)
    to = iota(shape, 1)
    gap = iota((tokens, 1), 0) + back * tokens - to
    first = (back - rank_ref[0]) * tokens
    allowed = (gap >= 0) & (gap < ROW) & (to >= first)
    outs = []
    for h in range(heads):
        mine = slice(h * tokens, (h + 1) * tokens)

        def window(kind):
            return jnp.concatenate(
                [
                    c_ref[kind, mine],
                    b_ref[1, kind, mine],
                    a_ref[kind, mine],
                    b_ref[0, kind, mine],
                    pair_ref[kind, mine],
                ],
                axis=0,
            )

        out, dq, *pair = attend(query_ref[mine], window(0), window(1), g_ref[mine], allowed, scale)
        outs.append(out)
        dq_mem[mine] = dq.astype(BF16)
        for kind, value in enumerate(pair):
            four, three, two, one, mid = [
                value[j * tokens : (j + 1) * tokens].astype(BF16) for j in range(back + 1)
            ]
            mid_mem[kind, mine] = mid
            two_mem[kind, mine] = two
            one_three_ref[0, kind, mine] = one
            one_three_ref[1, kind, mine] = three
            four_ref[kind, mine] = four
    attended_mem[...] = jnp.concatenate(outs, axis=1)
    pairs = (
        (attended_mem, attended_ref),
        (dq_mem, dq_ref),
        (mid_mem, mid_ref),
        (two_mem, two_ref),
    )
    stores = [pltpu.make_async_copy(m, r, sems.at[n]) for n, (m, r) in enumerate(pairs)]
    for store in stores:
        store.start()
    for store in stores:
        store.wait()


def combine_kernel(two_ref, d_ref, out_ref, two_mem, sem):
    load = pltpu.make_async_copy(two_ref, two_mem, sem.at[0])
    load.start()
    load.wait()
    out_ref[...] = (two_mem[...].astype(F32) + d_ref[1].astype(F32)).astype(BF16)


def project_kernel(heads, attended_ref, back_ref, w_ref, out_ref, attended_mem, sem):
    load = pltpu.make_async_copy(attended_ref, attended_mem, sem.at[0])
    load.start()
    half = attended_ref.shape[1]
    lines, _, span, hd = back_ref.shape
    parts, _, width = out_ref.shape
    strided = by_token(back_ref[:, 0].astype(F32).reshape(lines * span, hd).astype(BF16), heads)
    cols = [slice(p * width, (p + 1) * width) for p in range(parts)]
    sums = [mm(strided, w_ref[half:, c]) for c in cols]
    load.wait()
    for p, c in enumerate(cols):
        out_ref[p] = (sums[p] + mm(attended_mem[...], w_ref[:half, c])).astype(BF16)


def finish_kernel(
    heads, sums_ref, dq_ref, mid_ref, d_ref, e_ref, f_ref, back_ref, mixed_ref, grads_ref
):
    mixed_ref[...] = sum(sums_ref[p].astype(F32) for p in range(sums_ref.shape[0])).astype(BF16)
    rows, hd = dq_ref.shape
    pieces = [dq_ref[...]]
    for kind in range(2):
        total = mid_ref[kind].astype(F32) + d_ref[0, kind].astype(F32)
        total = total + e_ref[kind].astype(F32) + f_ref[kind].astype(F32)
        pieces.append(total.astype(BF16))
    joined = mm_tn(places(rows, heads), jnp.concatenate(pieces, axis=1)).astype(BF16)
    for kind in range(3):
        grads_ref[0, kind] = joined[:, kind * hd : (kind + 1) * hd]
        grads_ref[1, kind] = back_ref[:, 1 + kind].astype(F32).reshape(rows, hd).astype(BF16)


def call(kernel, outs, *args, far=(), away=(), scratch=()):
    vmem, smem, hbm = [pl.BlockSpec(memory_space=m) for m in (pltpu.VMEM, pltpu.SMEM, pltpu.HBM)]
    ins = [smem if a.dtype == jnp.int32 else hbm if n in far else vmem for n, a in enumerate(args)]
    args = [
        pltpu.with_memory_space_constraint(a, pltpu.HBM) if n in far else a
        for n, a in enumerate(args)
    ]
    made = [(pltpu.HBM if n in away else jax.ShapeDtypeStruct)(*o) for n, o in enumerate(outs)]
    return pl.pallas_call(
        kernel,
        out_shape=made,
        in_specs=ins,
        out_specs=[hbm if n in away else vmem for n in range(len(outs))],
        scratch_shapes=[
            pltpu.VMEM(*s) if isinstance(s, tuple) else pltpu.SemaphoreType.DMA((s,)) for s in scratch
        ],
        compiler_params=pltpu.CompilerParams(vmem_limit_bytes=SCRATCH),
    )(*args)


def layer(qkv, out_weight, out_grad):
    _, _, tokens, heads, hd = qkv.shape
    lines = lax.axis_size("line")
    quarters = lax.axis_size("quarter")
    parts = lax.axis_size("head")
    seq = ("line", "quarter")
    count = lines * quarters
    rank = (lax.axis_index("line") * quarters + lax.axis_index("quarter")).astype(jnp.int32)
    scale = 1.0 / math.sqrt(hd)
    rows = tokens * heads
    span = rows // lines
    width = out_grad.shape[1]
    kernel = functools.partial

    def shifted(value, steps):
        pairs = [(i, i + steps) for i in range(count) if 0 <= i + steps < count]
        return lax.ppermute(value, seq, pairs)

    x = qkv.reshape(2, 3, rows, hd)
    w = out_weight.reshape(2 * heads * hd, parts * width)

    flat, pair_of, wide = (rows, hd), (2, rows, hd), (tokens, heads * hd)
    pair, query = call(
        kernel(split_kernel, heads),
        [(pair_of, BF16), (flat, BF16)],
        x,
        far=(0,),
        scratch=(((3, *flat), BF16), 1),
    )
    a = shifted(pair, 2)
    og = lax.all_gather(out_grad, "head", axis=0)
    both = jnp.stack([pair, a])
    b = shifted(both, 1)
    c = shifted(a, 2)
    (send,) = call(
        kernel(grad_heads_kernel, heads),
        [((lines, 4, span, hd), BF16)],
        og,
        w,
        x,
        far=(1, 2),
        scratch=(((parts, heads * hd, width), BF16), ((3, rows, hd), BF16), parts + 1),
    )
    got = lax.all_to_all(send, "line", 0, 0, tiled=True)
    flat, pair_of = (rows, hd), (2, rows, hd)
    (g_local,) = call(kernel(local_grad_kernel, heads), [(flat, BF16)], og, w)
    away = (wide, flat, pair_of, pair_of)
    one_three, four, attended, local_dq, mid, two = call(
        kernel(local_kernel, heads, scale),
        [(o, BF16) for o in ((2, *pair_of), pair_of, *away)],
        rank.reshape(1),
        query,
        pair,
        g_local,
        a,
        b,
        c,
        away=(2, 3, 4, 5),
        scratch=(*((o, BF16) for o in away), len(away)),
    )
    d = shifted(one_three, -1)
    e = shifted(four, -4)
    (results,) = call(kernel(strided_kernel, scale), [(got.shape, BF16)], got)
    returned = lax.all_to_all(results, "line", 0, 0, tiled=True)
    (twos,) = call(
        combine_kernel, [(pair_of, BF16)], two, d, far=(0,), scratch=((pair_of, BF16), 1)
    )
    f = shifted(twos, -2)
    (partial,) = call(
        kernel(project_kernel, heads),
        [((parts, tokens, width), BF16)],
        attended,
        returned,
        w,
        far=(0,),
        scratch=((wide, BF16), 1),
    )
    sums = lax.all_to_all(partial, "head", 0, 0, tiled=True)
    mixed, grads = call(
        kernel(finish_kernel, heads),
        [((tokens, width), BF16), ((2, 3, rows, hd), BF16)],
        sums,
        local_dq,
        mid,
        d,
        e,
        f,
        returned,
    )
    return mixed, grads.reshape(qkv.shape)


def solution(mesh):
    count = mesh.shape["seq"]
    split = Mesh(
        mesh.devices.reshape(count // 4, 4, mesh.shape["head"]), ("line", "quarter", "head")
    )
    seq = ("line", "quarter")
    return jax.shard_map(
        layer,
        mesh=split,
        in_specs=(
            P(None, None, seq, "head", None),
            P(None, "head", None, None),
            P(seq, "head"),
        ),
        out_specs=(P(seq, "head"), P(None, None, seq, "head", None)),
        check_vma=False,
    )
```

```python
import functools
import math

import jax
import jax.numpy as jnp
from jax import lax
from jax.experimental import pallas as pl
from jax.experimental.pallas import tpu as pltpu
from jax.sharding import Mesh
from jax.sharding import PartitionSpec as P

ROW = 512
SCRATCH = 24 * 2**20
F32 = jnp.float32
BF16 = jnp.bfloat16


def dot(a, b, dims):
    return lax.dot_general(a, b, (dims, ((), ())), preferred_element_type=F32)


def mm(a, b):
    return dot(a, b, ((1,), (0,)))


def mm_nt(a, b):
    return dot(a, b, ((1,), (1,)))


def mm_tn(a, b):
    return dot(a, b, ((0,), (0,)))


def iota(shape, axis):
    return lax.broadcasted_iota(jnp.int32, shape, axis)


def forward(q, k, v, allowed, scale):
    scores = jnp.where(allowed, mm_nt(q, k) * scale, -jnp.inf)
    largest = jnp.max(scores, axis=1, keepdims=True)
    raised = jnp.exp(scores - largest)
    probs = raised * (1.0 / jnp.sum(raised, axis=1, keepdims=True))
    return probs, probs.astype(BF16), mm(probs.astype(BF16), v).astype(BF16)


def score_grads(probs, out, v, g):
    delta = jnp.sum(g.astype(F32) * out.astype(F32), axis=1, keepdims=True)
    return (probs * (mm_nt(g, v) - delta)).astype(BF16)


def attend(q, k, v, g, allowed, scale):
    probs, rounded, out = forward(q, k, v, allowed, scale)
    gs = score_grads(probs, out, v, g)
    return out, mm(gs, k) * scale, mm_tn(gs, q) * scale, mm_tn(rounded, g)


def rows_of(g, rows, heads, hd, tokens):
    total = 0
    for h in range(heads):
        pick = iota((rows, tokens), 0) == heads * iota((rows, tokens), 1) + h
        total = total + mm_nt(pick.astype(BF16), g[h * hd : (h + 1) * hd])
    return total


def grad_heads_kernel(heads, og_ref, w_ref, x_ref, send_ref):
    lines, _, span, hd = send_ref.shape
    parts, tokens, _ = og_ref.shape
    g = sum(mm_nt(w_ref[p], og_ref[p]) for p in range(parts))
    g = rows_of(g.astype(BF16), lines * span, heads, hd, tokens)
    send_ref[:, 3] = g.reshape(lines, span, hd).astype(BF16)
    for kind in range(3):
        send_ref[:, kind] = x_ref[kind].astype(F32).reshape(lines, span, hd).astype(BF16)


def strided_kernel(scale, in_ref, out_ref):
    lines, _, span, hd = in_ref.shape
    rows = lines * span

    def part(kind):
        return in_ref[:, kind].astype(F32).reshape(rows, hd).astype(BF16)

    at, to = iota((rows, rows), 0), iota((rows, rows), 1)
    allowed = (at >= to) & (at % span == to % span)
    results = attend(part(0), part(1), part(2), part(3), allowed, scale)
    for kind, value in enumerate(results):
        out_ref[:, kind] = value.astype(F32).reshape(lines, span, hd).astype(BF16)


def by_token(value, heads):
    rows, _ = value.shape
    shape = (rows // heads, rows)
    picks = [iota(shape, 1) == heads * iota(shape, 0) + h for h in range(heads)]
    return jnp.concatenate([mm(p.astype(BF16), value).astype(BF16) for p in picks], axis=1)


def places(rows, heads):
    tokens = rows // heads
    at = iota((rows, 1), 0)
    return (iota((rows, rows), 1) == at % tokens * heads + at // tokens).astype(BF16)


def split_kernel(heads, x_ref, w_ref, pair_ref, query_ref, w_out, x_out, x_mem, sems):
    parts, half, width = w_out.shape
    load = pltpu.make_async_copy(x_ref.at[0], x_mem, sems.at[0])
    others = [pltpu.make_async_copy(x_ref.at[1], x_out, sems.at[1])]
    for p in range(parts):
        cols = slice(p * width, (p + 1) * width)
        others.append(pltpu.make_async_copy(w_ref.at[half:, cols], w_out.at[p], sems.at[2 + p]))
    load.start()
    for other in others:
        other.start()
    rows, hd = query_ref.shape
    apart = places(rows, heads)
    load.wait()
    whole = mm(apart, jnp.concatenate([x_mem[k] for k in range(3)], axis=1)).astype(BF16)
    query_ref[...] = whole[:, :hd]
    pair_ref[0] = whole[:, hd : 2 * hd]
    pair_ref[1] = whole[:, 2 * hd :]
    for other in others:
        other.wait()


def local_grad_kernel(heads, og_ref, w_ref, g_ref):
    parts, tokens, width = og_ref.shape
    hd = g_ref.shape[1]
    g = sum(
        mm_nt(w_ref[: heads * hd, p * width : (p + 1) * width], og_ref[p]) for p in range(parts)
    ).astype(BF16)
    same = (iota((tokens, tokens), 0) == iota((tokens, tokens), 1)).astype(BF16)
    for h in range(heads):
        own = mm_nt(same, g[h * hd : (h + 1) * hd])
        g_ref[h * tokens : (h + 1) * tokens] = own.astype(BF16)


def local_kernel(
    heads, scale, rank_ref, query_ref, pair_ref, g_ref, a_ref, b_ref, c_ref,
    one_three_ref, four_ref, attended_ref, dq_ref, mid_ref, two_ref,
    attended_mem, dq_mem, mid_mem, two_mem, sems,
):
    rows, _ = dq_ref.shape
    tokens = rows // heads
    back = ROW // tokens
    shape = (tokens, (back + 1) * tokens)
    to = iota(shape, 1)
    gap = iota((tokens, 1), 0) + back * tokens - to
    first = (back - rank_ref[0]) * tokens
    allowed = (gap >= 0) & (gap < ROW) & (to >= first)
    pairs = (
        (attended_mem, attended_ref),
        (dq_mem, dq_ref),
        (mid_mem, mid_ref),
        (two_mem, two_ref),
    )
    stores = [pltpu.make_async_copy(m, r, sems.at[n]) for n, (m, r) in enumerate(pairs)]
    slices = [slice(h * tokens, (h + 1) * tokens) for h in range(heads)]

    def window(kind, mine):
        refs = (c_ref, b_ref.at[1], a_ref, b_ref.at[0], pair_ref)
        return jnp.concatenate([r[kind, mine] for r in refs], axis=0)

    keys = [window(0, mine) for mine in slices]
    values = [window(1, mine) for mine in slices]
    ran = [
        forward(query_ref[mine], k, v, allowed, scale) for mine, k, v in zip(slices, keys, values)
    ]
    attended_mem[...] = jnp.concatenate([r[2] for r in ran], axis=1)
    stores[0].start()
    grads = [
        score_grads(r[0], r[2], v, g_ref[mine]) for mine, r, v in zip(slices, ran, values)
    ]

    def block(j, h, kind):
        cols = slice(j * tokens, (j + 1) * tokens)
        if kind == 0:
            return (mm_tn(grads[h][:, cols], query_ref[slices[h]]) * scale).astype(BF16)
        return mm_tn(ran[h][1][:, cols], g_ref[slices[h]]).astype(BF16)

    for h, mine in enumerate(slices):
        for kind in range(2):
            mid_mem[kind, mine] = block(back, h, kind)
            two_mem[kind, mine] = block(back - 2, h, kind)
    stores[2].start()
    stores[3].start()
    for h, mine in enumerate(slices):
        dq_mem[mine] = (mm(grads[h], keys[h]) * scale).astype(BF16)
    stores[1].start()
    for h, mine in enumerate(slices):
        for kind in range(2):
            one_three_ref[0, kind, mine] = block(back - 1, h, kind)
            one_three_ref[1, kind, mine] = block(back - 3, h, kind)
            four_ref[kind, mine] = block(back - 4, h, kind)
    for store in stores:
        store.wait()


def combine_kernel(two_ref, d_ref, out_ref, two_mem, sem):
    load = pltpu.make_async_copy(two_ref, two_mem, sem.at[0])
    load.start()
    load.wait()
    out_ref[...] = (two_mem[...].astype(F32) + d_ref[1].astype(F32)).astype(BF16)


def project_kernel(heads, attended_ref, back_ref, w_ref, out_ref, attended_mem, sem):
    load = pltpu.make_async_copy(attended_ref, attended_mem, sem.at[0])
    load.start()
    half = attended_ref.shape[1]
    lines, _, span, hd = back_ref.shape
    parts, _, width = out_ref.shape
    strided = by_token(back_ref[:, 0].astype(F32).reshape(lines * span, hd).astype(BF16), heads)
    cols = [slice(p * width, (p + 1) * width) for p in range(parts)]
    sums = [mm(strided, w_ref[half:, c]) for c in cols]
    load.wait()
    for p, c in enumerate(cols):
        out_ref[p] = (sums[p] + mm(attended_mem[...], w_ref[:half, c])).astype(BF16)


def finish_kernel(
    heads, sums_ref, dq_ref, mid_ref, d_ref, e_ref, f_ref, back_ref, mixed_ref, grads_ref
):
    mixed_ref[...] = sum(sums_ref[p].astype(F32) for p in range(sums_ref.shape[0])).astype(BF16)
    rows, hd = dq_ref.shape
    pieces = [dq_ref[...]]
    for kind in range(2):
        total = mid_ref[kind].astype(F32) + d_ref[0, kind].astype(F32)
        total = total + e_ref[kind].astype(F32) + f_ref[kind].astype(F32)
        pieces.append(total.astype(BF16))
    joined = mm_tn(places(rows, heads), jnp.concatenate(pieces, axis=1)).astype(BF16)
    for kind in range(3):
        grads_ref[0, kind] = joined[:, kind * hd : (kind + 1) * hd]
        grads_ref[1, kind] = back_ref[:, 1 + kind].astype(F32).reshape(rows, hd).astype(BF16)


def call(kernel, outs, *args, far=(), away=(), scratch=()):
    vmem, smem, hbm = [pl.BlockSpec(memory_space=m) for m in (pltpu.VMEM, pltpu.SMEM, pltpu.HBM)]
    ins = [smem if a.dtype == jnp.int32 else hbm if n in far else vmem for n, a in enumerate(args)]
    args = [
        pltpu.with_memory_space_constraint(a, pltpu.HBM) if n in far else a
        for n, a in enumerate(args)
    ]
    made = [(pltpu.HBM if n in away else jax.ShapeDtypeStruct)(*o) for n, o in enumerate(outs)]
    return pl.pallas_call(
        kernel,
        out_shape=made,
        in_specs=ins,
        out_specs=[hbm if n in away else vmem for n in range(len(outs))],
        scratch_shapes=[
            pltpu.VMEM(*s) if isinstance(s, tuple) else pltpu.SemaphoreType.DMA((s,)) for s in scratch
        ],
        compiler_params=pltpu.CompilerParams(vmem_limit_bytes=SCRATCH),
    )(*args)


def layer(qkv, out_weight, out_grad):
    _, _, tokens, heads, hd = qkv.shape
    lines = lax.axis_size("line")
    quarters = lax.axis_size("quarter")
    parts = lax.axis_size("head")
    seq = ("line", "quarter")
    count = lines * quarters
    rank = (lax.axis_index("line") * quarters + lax.axis_index("quarter")).astype(jnp.int32)
    scale = 1.0 / math.sqrt(hd)
    rows = tokens * heads
    span = rows // lines
    width = out_grad.shape[1]
    kernel = functools.partial

    def shifted(value, steps):
        pairs = [(i, i + steps) for i in range(count) if 0 <= i + steps < count]
        return lax.ppermute(value, seq, pairs)

    x = qkv.reshape(2, 3, rows, hd)
    w = out_weight.reshape(2 * heads * hd, parts * width)

    flat, pair_of, wide = (rows, hd), (2, rows, hd), (tokens, heads * hd)
    pair, query, w_strided, x_strided = call(
        kernel(split_kernel, heads),
        [
            (pair_of, BF16),
            (flat, BF16),
            ((parts, heads * hd, width), BF16),
            ((3, *flat), BF16),
        ],
        x,
        w,
        far=(0, 1),
        scratch=(((3, *flat), BF16), 2 + parts),
    )
    a = shifted(pair, 2)
    og = lax.all_gather(out_grad, "head", axis=0)
    both = jnp.stack([pair, a])
    b = shifted(both, 1)
    c = shifted(a, 2)
    (send,) = call(
        kernel(grad_heads_kernel, heads), [((lines, 4, span, hd), BF16)], og, w_strided, x_strided
    )
    got = lax.all_to_all(send, "line", 0, 0, tiled=True)
    flat, pair_of = (rows, hd), (2, rows, hd)
    (g_local,) = call(kernel(local_grad_kernel, heads), [(flat, BF16)], og, w)
    away = (wide, flat, pair_of, pair_of)
    one_three, four, attended, local_dq, mid, two = call(
        kernel(local_kernel, heads, scale),
        [(o, BF16) for o in ((2, *pair_of), pair_of, *away)],
        rank.reshape(1),
        query,
        pair,
        g_local,
        a,
        b,
        c,
        away=(2, 3, 4, 5),
        scratch=(*((o, BF16) for o in away), len(away)),
    )
    d = shifted(one_three, -1)
    e = shifted(four, -4)
    (results,) = call(kernel(strided_kernel, scale), [(got.shape, BF16)], got)
    returned = lax.all_to_all(results, "line", 0, 0, tiled=True)
    (twos,) = call(
        combine_kernel, [(pair_of, BF16)], two, d, far=(0,), scratch=((pair_of, BF16), 1)
    )
    f = shifted(twos, -2)
    (partial,) = call(
        kernel(project_kernel, heads),
        [((parts, tokens, width), BF16)],
        attended,
        returned,
        w,
        far=(0,),
        scratch=((wide, BF16), 1),
    )
    sums = lax.all_to_all(partial, "head", 0, 0, tiled=True)
    mixed, grads = call(
        kernel(finish_kernel, heads),
        [((tokens, width), BF16), ((2, 3, rows, hd), BF16)],
        sums,
        local_dq,
        mid,
        d,
        e,
        f,
        returned,
    )
    return mixed, grads.reshape(qkv.shape)


def solution(mesh):
    count = mesh.shape["seq"]
    split = Mesh(
        mesh.devices.reshape(count // 4, 4, mesh.shape["head"]), ("line", "quarter", "head")
    )
    seq = ("line", "quarter")
    return jax.shard_map(
        layer,
        mesh=split,
        in_specs=(
            P(None, None, seq, "head", None),
            P(None, "head", None, None),
            P(seq, "head"),
        ),
        out_specs=(P(seq, "head"), P(None, None, seq, "head", None)),
        check_vma=False,
    )
```

```python
import functools
import math

import jax
import jax.numpy as jnp
from jax import lax
from jax.experimental import pallas as pl
from jax.experimental.pallas import tpu as pltpu
from jax.sharding import Mesh
from jax.sharding import PartitionSpec as P

ROW = 512
SCRATCH = 24 * 2**20
F32 = jnp.float32
BF16 = jnp.bfloat16


def dot(a, b, dims):
    return lax.dot_general(a, b, (dims, ((), ())), preferred_element_type=F32)


def mm(a, b):
    return dot(a, b, ((1,), (0,)))


def mm_nt(a, b):
    return dot(a, b, ((1,), (1,)))


def mm_tn(a, b):
    return dot(a, b, ((0,), (0,)))


def iota(shape, axis):
    return lax.broadcasted_iota(jnp.int32, shape, axis)


def forward(q, k, v, allowed, scale):
    scores = jnp.where(allowed, mm_nt(q, k) * scale, -jnp.inf)
    largest = jnp.max(scores, axis=1, keepdims=True)
    raised = jnp.exp(scores - largest)
    probs = raised * (1.0 / jnp.sum(raised, axis=1, keepdims=True))
    return probs, probs.astype(BF16), mm(probs.astype(BF16), v).astype(BF16)


def score_grads(probs, out, v, g):
    delta = jnp.sum(g.astype(F32) * out.astype(F32), axis=1, keepdims=True)
    return (probs * (mm_nt(g, v) - delta)).astype(BF16)


def attend(q, k, v, g, allowed, scale):
    probs, rounded, out = forward(q, k, v, allowed, scale)
    gs = score_grads(probs, out, v, g)
    return out, mm(gs, k) * scale, mm_tn(gs, q) * scale, mm_tn(rounded, g)


def rows_of(g, rows, heads, hd, tokens):
    total = 0
    for h in range(heads):
        pick = iota((rows, tokens), 0) == heads * iota((rows, tokens), 1) + h
        total = total + mm_nt(pick.astype(BF16), g[h * hd : (h + 1) * hd])
    return total


def grad_heads_kernel(heads, og_ref, w_ref, x_ref, send_ref):
    lines, _, span, hd = send_ref.shape
    parts, tokens, _ = og_ref.shape
    g = sum(mm_nt(w_ref[p], og_ref[p]) for p in range(parts))
    g = rows_of(g.astype(BF16), lines * span, heads, hd, tokens)
    send_ref[:, 3] = g.reshape(lines, span, hd).astype(BF16)
    for kind in range(3):
        send_ref[:, kind] = x_ref[kind].astype(F32).reshape(lines, span, hd).astype(BF16)


def strided_kernel(scale, in_ref, out_ref):
    lines, _, span, hd = in_ref.shape
    rows = lines * span

    def part(kind):
        return in_ref[:, kind].astype(F32).reshape(rows, hd).astype(BF16)

    at, to = iota((rows, rows), 0), iota((rows, rows), 1)
    allowed = (at >= to) & (at % span == to % span)
    results = attend(part(0), part(1), part(2), part(3), allowed, scale)
    for kind, value in enumerate(results):
        out_ref[:, kind] = value.astype(F32).reshape(lines, span, hd).astype(BF16)


def by_token(value, heads):
    rows, _ = value.shape
    shape = (rows // heads, rows)
    picks = [iota(shape, 1) == heads * iota(shape, 0) + h for h in range(heads)]
    return jnp.concatenate([mm(p.astype(BF16), value).astype(BF16) for p in picks], axis=1)


def places(rows, heads):
    tokens = rows // heads
    at = iota((rows, 1), 0)
    return (iota((rows, rows), 1) == at % tokens * heads + at // tokens).astype(BF16)


def split_kernel(heads, x_ref, w_ref, pair_ref, query_ref, w_out, x_out, x_mem, sems):
    parts, half, width = w_out.shape
    load = pltpu.make_async_copy(x_ref.at[0], x_mem, sems.at[0])
    others = [pltpu.make_async_copy(x_ref.at[1], x_out, sems.at[1])]
    for p in range(parts):
        cols = slice(p * width, (p + 1) * width)
        others.append(pltpu.make_async_copy(w_ref.at[half:, cols], w_out.at[p], sems.at[2 + p]))
    load.start()
    for other in others:
        other.start()
    rows, hd = query_ref.shape
    apart = places(rows, heads)
    load.wait()
    whole = mm(apart, jnp.concatenate([x_mem[k] for k in range(3)], axis=1)).astype(BF16)
    query_ref[...] = whole[:, :hd]
    pair_ref[0] = whole[:, hd : 2 * hd]
    pair_ref[1] = whole[:, 2 * hd :]
    for other in others:
        other.wait()


def local_grad_kernel(heads, og_ref, w_ref, pair_ref, a_ref, g_ref, both_ref, sem):
    load = pltpu.make_async_copy(pair_ref, both_ref.at[0], sem.at[0])
    load.start()
    both_ref[1] = a_ref[...]
    parts, tokens, width = og_ref.shape
    hd = g_ref.shape[1]
    g = sum(
        mm_nt(w_ref[: heads * hd, p * width : (p + 1) * width], og_ref[p]) for p in range(parts)
    ).astype(BF16)
    same = (iota((tokens, tokens), 0) == iota((tokens, tokens), 1)).astype(BF16)
    for h in range(heads):
        own = mm_nt(same, g[h * hd : (h + 1) * hd])
        g_ref[h * tokens : (h + 1) * tokens] = own.astype(BF16)
    load.wait()


def local_kernel(
    heads, scale, rank_ref, query_ref, pair_ref, g_ref, a_ref, b_ref, c_ref,
    one_three_ref, four_ref, attended_ref, dq_ref, mid_ref, two_ref,
    attended_mem, dq_mem, mid_mem, two_mem, sems,
):
    rows, _ = dq_ref.shape
    tokens = rows // heads
    back = ROW // tokens
    shape = (tokens, (back + 1) * tokens)
    to = iota(shape, 1)
    gap = iota((tokens, 1), 0) + back * tokens - to
    first = (back - rank_ref[0]) * tokens
    allowed = (gap >= 0) & (gap < ROW) & (to >= first)
    pairs = (
        (attended_mem, attended_ref),
        (dq_mem, dq_ref),
        (mid_mem, mid_ref),
        (two_mem, two_ref),
    )
    stores = [pltpu.make_async_copy(m, r, sems.at[n]) for n, (m, r) in enumerate(pairs)]
    slices = [slice(h * tokens, (h + 1) * tokens) for h in range(heads)]

    def window(kind, mine):
        refs = (c_ref, b_ref.at[1], a_ref, b_ref.at[0], pair_ref)
        return jnp.concatenate([r[kind, mine] for r in refs], axis=0)

    keys = [window(0, mine) for mine in slices]
    values = [window(1, mine) for mine in slices]
    ran = [
        forward(query_ref[mine], k, v, allowed, scale) for mine, k, v in zip(slices, keys, values)
    ]
    attended_mem[...] = jnp.concatenate([r[2] for r in ran], axis=1)
    stores[0].start()
    grads = [
        score_grads(r[0], r[2], v, g_ref[mine]) for mine, r, v in zip(slices, ran, values)
    ]

    def block(j, h, kind):
        cols = slice(j * tokens, (j + 1) * tokens)
        if kind == 0:
            return (mm_tn(grads[h][:, cols], query_ref[slices[h]]) * scale).astype(BF16)
        return mm_tn(ran[h][1][:, cols], g_ref[slices[h]]).astype(BF16)

    for h, mine in enumerate(slices):
        for kind in range(2):
            mid_mem[kind, mine] = block(back, h, kind)
            two_mem[kind, mine] = block(back - 2, h, kind)
    stores[2].start()
    stores[3].start()
    for h, mine in enumerate(slices):
        dq_mem[mine] = (mm(grads[h], keys[h]) * scale).astype(BF16)
    stores[1].start()
    for h, mine in enumerate(slices):
        for kind in range(2):
            one_three_ref[0, kind, mine] = block(back - 1, h, kind)
            one_three_ref[1, kind, mine] = block(back - 3, h, kind)
            four_ref[kind, mine] = block(back - 4, h, kind)
    for store in stores:
        store.wait()


def combine_kernel(two_ref, d_ref, out_ref, two_mem, sem):
    load = pltpu.make_async_copy(two_ref, two_mem, sem.at[0])
    load.start()
    load.wait()
    out_ref[...] = (two_mem[...].astype(F32) + d_ref[1].astype(F32)).astype(BF16)


def project_kernel(heads, attended_ref, back_ref, w_ref, out_ref, attended_mem, sem):
    load = pltpu.make_async_copy(attended_ref, attended_mem, sem.at[0])
    load.start()
    half = attended_ref.shape[1]
    lines, _, span, hd = back_ref.shape
    parts, _, width = out_ref.shape
    strided = by_token(back_ref[:, 0].astype(F32).reshape(lines * span, hd).astype(BF16), heads)
    cols = [slice(p * width, (p + 1) * width) for p in range(parts)]
    sums = [mm(strided, w_ref[half:, c]) for c in cols]
    load.wait()
    for p, c in enumerate(cols):
        out_ref[p] = (sums[p] + mm(attended_mem[...], w_ref[:half, c])).astype(BF16)


def finish_kernel(
    heads, sums_ref, dq_ref, mid_ref, d_ref, e_ref, f_ref, back_ref, mixed_ref, grads_ref
):
    mixed_ref[...] = sum(sums_ref[p].astype(F32) for p in range(sums_ref.shape[0])).astype(BF16)
    rows, hd = dq_ref.shape
    pieces = [dq_ref[...]]
    for kind in range(2):
        total = mid_ref[kind].astype(F32) + d_ref[0, kind].astype(F32)
        total = total + e_ref[kind].astype(F32) + f_ref[kind].astype(F32)
        pieces.append(total.astype(BF16))
    joined = mm_tn(places(rows, heads), jnp.concatenate(pieces, axis=1)).astype(BF16)
    for kind in range(3):
        grads_ref[0, kind] = joined[:, kind * hd : (kind + 1) * hd]
        grads_ref[1, kind] = back_ref[:, 1 + kind].astype(F32).reshape(rows, hd).astype(BF16)


def call(kernel, outs, *args, far=(), away=(), scratch=()):
    vmem, smem, hbm = [pl.BlockSpec(memory_space=m) for m in (pltpu.VMEM, pltpu.SMEM, pltpu.HBM)]
    ins = [smem if a.dtype == jnp.int32 else hbm if n in far else vmem for n, a in enumerate(args)]
    args = [
        pltpu.with_memory_space_constraint(a, pltpu.HBM) if n in far else a
        for n, a in enumerate(args)
    ]
    made = [(pltpu.HBM if n in away else jax.ShapeDtypeStruct)(*o) for n, o in enumerate(outs)]
    return pl.pallas_call(
        kernel,
        out_shape=made,
        in_specs=ins,
        out_specs=[hbm if n in away else vmem for n in range(len(outs))],
        scratch_shapes=[
            pltpu.VMEM(*s) if isinstance(s, tuple) else pltpu.SemaphoreType.DMA((s,)) for s in scratch
        ],
        compiler_params=pltpu.CompilerParams(vmem_limit_bytes=SCRATCH),
    )(*args)


def layer(qkv, out_weight, out_grad):
    _, _, tokens, heads, hd = qkv.shape
    lines = lax.axis_size("line")
    quarters = lax.axis_size("quarter")
    parts = lax.axis_size("head")
    seq = ("line", "quarter")
    count = lines * quarters
    rank = (lax.axis_index("line") * quarters + lax.axis_index("quarter")).astype(jnp.int32)
    scale = 1.0 / math.sqrt(hd)
    rows = tokens * heads
    span = rows // lines
    width = out_grad.shape[1]
    kernel = functools.partial

    def shifted(value, steps):
        pairs = [(i, i + steps) for i in range(count) if 0 <= i + steps < count]
        return lax.ppermute(value, seq, pairs)

    x = qkv.reshape(2, 3, rows, hd)
    w = out_weight.reshape(2 * heads * hd, parts * width)

    flat, pair_of, wide = (rows, hd), (2, rows, hd), (tokens, heads * hd)
    pair, query, w_strided, x_strided = call(
        kernel(split_kernel, heads),
        [
            (pair_of, BF16),
            (flat, BF16),
            ((parts, heads * hd, width), BF16),
            ((3, *flat), BF16),
        ],
        x,
        w,
        far=(0, 1),
        scratch=(((3, *flat), BF16), 2 + parts),
    )
    a = shifted(pair, 2)
    og = lax.all_gather(out_grad, "head", axis=0)
    g_local, both = call(
        kernel(local_grad_kernel, heads),
        [(flat, BF16), ((2, *pair_of), BF16)],
        og,
        w,
        pair,
        a,
        far=(2,),
        scratch=(1,),
    )
    b = shifted(both, 1)
    c = shifted(a, 2)
    (send,) = call(
        kernel(grad_heads_kernel, heads), [((lines, 4, span, hd), BF16)], og, w_strided, x_strided
    )
    got = lax.all_to_all(send, "line", 0, 0, tiled=True)
    flat, pair_of = (rows, hd), (2, rows, hd)
    away = (wide, flat, pair_of, pair_of)
    one_three, four, attended, local_dq, mid, two = call(
        kernel(local_kernel, heads, scale),
        [(o, BF16) for o in ((2, *pair_of), pair_of, *away)],
        rank.reshape(1),
        query,
        pair,
        g_local,
        a,
        b,
        c,
        away=(2, 3, 4, 5),
        scratch=(*((o, BF16) for o in away), len(away)),
    )
    d = shifted(one_three, -1)
    e = shifted(four, -4)
    (results,) = call(kernel(strided_kernel, scale), [(got.shape, BF16)], got)
    returned = lax.all_to_all(results, "line", 0, 0, tiled=True)
    (twos,) = call(
        combine_kernel, [(pair_of, BF16)], two, d, far=(0,), scratch=((pair_of, BF16), 1)
    )
    f = shifted(twos, -2)
    (partial,) = call(
        kernel(project_kernel, heads),
        [((parts, tokens, width), BF16)],
        attended,
        returned,
        w,
        far=(0,),
        scratch=((wide, BF16), 1),
    )
    sums = lax.all_to_all(partial, "head", 0, 0, tiled=True)
    mixed, grads = call(
        kernel(finish_kernel, heads),
        [((tokens, width), BF16), ((2, 3, rows, hd), BF16)],
        sums,
        local_dq,
        mid,
        d,
        e,
        f,
        returned,
    )
    return mixed, grads.reshape(qkv.shape)


def solution(mesh):
    count = mesh.shape["seq"]
    split = Mesh(
        mesh.devices.reshape(count // 4, 4, mesh.shape["head"]), ("line", "quarter", "head")
    )
    seq = ("line", "quarter")
    return jax.shard_map(
        layer,
        mesh=split,
        in_specs=(
            P(None, None, seq, "head", None),
            P(None, "head", None, None),
            P(seq, "head"),
        ),
        out_specs=(P(seq, "head"), P(None, None, seq, "head", None)),
        check_vma=False,
    )
```
